32 devices in a mesh: section: 2 (over x), fsdp: 16 (over z, y, core).
Axes of the slice: x: 2, y: 2, z: 4, core: 2. Of those that a mesh axis runs over, the one named last changes fastest.
Arguments:
- hidden_in: bfloat16 [16, 128, 4096], P('fsdp', 'section'), may hold values from -40 to 40
- queries: bfloat16 [2, 16, 128, 4096], P('section', 'fsdp'), may hold values from -260 to 260
- key_weight: bfloat16 [2, 4096, 512], P('section', 'fsdp'), may hold values from -0.09375 to 0.09375
- value_weight: bfloat16 [2, 4096, 512], P('section', 'fsdp'), may hold values from -0.09375 to 0.09375
- norm_gain: float32 [2, 4096], P('section'), may hold values from 0.5 to 1.5
Outputs:
- section_outputs: bfloat16 [2, 16, 128, 4096], P('section', 'fsdp')
The draws below stay inside these ranges and needn't reach their ends.
All inputs are finite; a program needn't handle non-finite values.
Results may differ from the reference program's by a relative error of at most 0.013.
Values may be sent and summed in bfloat16 or wider, within the bound.
A program may use at most 64 MiB of HBM per device.

```python
import math
import jax
import jax.numpy as jnp
from jax import lax

D = 4096
QH = 32
KVH = 4
HD = 128
TOK_DEV = 128
SECTIONS = 2
SEQS = 16


def draw_hidden_in(key, part):
    keys = jax.random.split(jax.random.fold_in(key, 11), 3)
    row_scale = jnp.exp(jax.random.uniform(keys[1], (SEQS, TOK_DEV, 1), jnp.float32, -1.15, 1.15))
    col_scale = jnp.exp(jax.random.uniform(keys[2], (SEQS, 1, D), jnp.float32, -1.15, 1.15))
    base = jnp.clip(jax.random.normal(keys[0], (SEQS, TOK_DEV, D), jnp.float32), -4.0, 4.0)
    return (base * row_scale * col_scale).astype(jnp.bfloat16)


def draw_queries(key, part):
    keys = jax.random.split(jax.random.fold_in(key, 23), 1)
    return jnp.clip(jax.random.normal(keys[0], (SECTIONS, SEQS, TOK_DEV, D), jnp.float32), -4.5, 4.5).astype(jnp.bfloat16)


def block_levels(rng, dims, cuts, low, largest):
    def one(axis_at, shards_of):
        heights = jax.random.uniform(jax.random.fold_in(jax.random.fold_in(rng, 6), axis_at), (shards_of,), jnp.float32, low / len(cuts), largest / len(cuts))
        return jnp.repeat(jnp.exp(heights), dims[axis_at] // shards_of).reshape((-1,) + (1,) * (len(dims) - axis_at - 1))

    factor_of = one(*cuts[0])
    for cut in cuts[1:]:
        factor_of = factor_of * one(*cut)
    return factor_of


def centred(rng, extent, scale, reach, cuts=(), kind=jnp.bfloat16):
    factor_of = block_levels(rng, extent, cuts, -0.22, 0.18) if cuts else 1.0
    values = jax.random.normal(rng, extent, jnp.float32) * scale * factor_of
    return jnp.minimum(jnp.maximum(values, -reach), reach).astype(kind)


def setup_inputs(seed: int = 0) -> dict:
    splits = jax.random.split(jax.random.key(seed), 6)
    hidden_in = draw_hidden_in(jax.random.fold_in(splits[5], 71), 0)
    queries = draw_queries(jax.random.fold_in(splits[5], 71), 0)
    key_weight = centred(splits[2], (SECTIONS, D, KVH * HD), D ** -0.5, 0.09375, ((0, 2), (1, 16)))
    value_weight = centred(splits[3], (SECTIONS, D, KVH * HD), D ** -0.5, 0.09375, ((0, 2), (1, 16)))
    norm_gain = jnp.clip(1.0 + 0.1 * jax.random.normal(splits[4], (SECTIONS, D), jnp.float32), 0.5, 1.5)
    return dict(hidden_in=hidden_in, queries=queries, key_weight=key_weight, value_weight=value_weight, norm_gain=norm_gain)


epsilon = 1e-05

def rms_norm(hidden, section_gain):
    hidden_f32 = hidden.astype(jnp.float32)
    mean_square = lax.optimization_barrier(jnp.mean(hidden_f32 * hidden_f32, axis=-1, keepdims=True))
    return (hidden_f32 * lax.rsqrt(mean_square + epsilon) * section_gain.astype(jnp.float32)).astype(jnp.bfloat16)

def rotate(heads, positions):
    half_width = heads.shape[-1] // 2
    frequency = jnp.exp(jnp.arange(half_width, dtype=jnp.float32) * (-2.0 * math.log(10000.0) / heads.shape[-1]))
    angles = positions[:, None] * frequency[None, :]
    cosine = jnp.cos(angles)[:, None, :]
    sine_table = jnp.sin(angles)[:, None, :]
    first_half = heads[..., :half_width]
    second_half = heads[..., half_width:]
    return jnp.concatenate([first_half * cosine - second_half * sine_table, second_half * cosine + first_half * sine_table], axis=-1)

def attend(query_heads, key_heads, value_heads, query_pos, key_pos):
    scores = jnp.einsum('lkgd,rkd->kglr', query_heads.astype(jnp.float32), key_heads.astype(jnp.float32))
    scores = scores * (1.0 / math.sqrt(HD))
    allowed = key_pos[None, :] <= query_pos[:, None]
    scores = jnp.where(allowed, scores, -1e+30)
    row_max = lax.optimization_barrier(jnp.max(scores, axis=-1, keepdims=True))
    weights = jnp.exp(scores - row_max)
    softmax_probs = (weights / lax.optimization_barrier(jnp.sum(weights, axis=-1, keepdims=True))).astype(jnp.bfloat16)
    attn_mixed = jnp.einsum('kglr,rkd->lkgd', softmax_probs.astype(jnp.float32), value_heads.astype(jnp.float32))
    return attn_mixed.reshape(query_heads.shape[0], -1)

def apply_layer(hidden, query_rows, key_proj, value_proj, section_gain):
    row_count = hidden.shape[0]
    positions = jnp.arange(row_count, dtype=jnp.float32)
    normed = rms_norm(hidden, section_gain)
    key_heads = jnp.dot(normed, key_proj, preferred_element_type=jnp.float32).reshape(row_count, KVH, HD)
    key_heads = rotate(key_heads, positions).astype(jnp.bfloat16)
    value_heads = jnp.dot(normed, value_proj, preferred_element_type=jnp.float32).astype(jnp.bfloat16).reshape(row_count, KVH, HD)
    query_heads = rotate(query_rows.astype(jnp.float32).reshape(row_count, QH, HD), positions).astype(jnp.bfloat16)
    query_heads = query_heads.reshape(row_count, KVH, QH // KVH, HD)
    attn_mixed = attend(query_heads, key_heads, value_heads, positions, positions)
    return (hidden.astype(jnp.float32) + attn_mixed).astype(jnp.bfloat16)

def reference(hidden_in, queries, key_weight, value_weight, norm_gain):

    def one_sequence(operands):
        hidden, query_seq = operands
        section_list = []
        for section_index in range(SECTIONS):
            hidden = apply_layer(hidden, query_seq[section_index], key_weight[section_index], value_weight[section_index], norm_gain[section_index])
            section_list.append(hidden)
        return jnp.stack(section_list)
    result = lax.map(one_sequence, (hidden_in, jnp.swapaxes(queries, 0, 1)))
    return jnp.swapaxes(result, 0, 1)
```

```python
import functools
import math

import jax
import jax.numpy as jnp
import numpy as np
from jax import lax
from jax.experimental import pallas as pl
from jax.experimental.pallas import tpu as pltpu
from jax.sharding import PartitionSpec as P

HD = 128
EPS = 1e-05
MESH = pl.DeviceIdType.MESH


def rope_tables(rows):
    half = HD // 2
    frequency = np.exp(np.arange(half, dtype=np.float32) * np.float32(-2.0 * math.log(10000.0) / HD))
    angles = np.arange(rows, dtype=np.float32)[:, None] * frequency[None, :].astype(np.float32)
    cosine, sine = np.cos(angles), np.sin(angles)
    return (
        np.concatenate([cosine, cosine], 1).astype(np.float32),
        np.concatenate([-sine, sine], 1).astype(np.float32),
    )


def rope(u, cosine, sine):
    return u * cosine + pltpu.roll(u, HD // 2, 1) * sine


def kernel(
    n, sections, outer, inner,
    hid, q_in, kw, vw, gain, cos_ref, sin_ref,
    out,
    w, xin, xs, qs, qp, normed, acc, kv, kvp,
    w_recv, w_send, own_sem, hid_recv, hid_send, hid_own, q_sem, kv_sem, x_sem,
):
    s = lax.axis_index("section")
    f = lax.axis_index("fsdp")
    core = lax.rem(f, 2)
    chip = f // 2
    i = lax.rem(chip, inner)
    o = chip // inner
    rows, width = xs.shape
    part = hid.shape[1]
    kvw = kw.shape[2]
    kv_heads = kvw // HD
    group = width // kvw
    depth = kw.shape[1]

    def index(oo, ii, cc):
        return (oo * inner + ii) * 2 + cc

    own_k = pltpu.make_async_copy(kw.at[0], w.at[f, 0], own_sem.at[0])
    own_v = pltpu.make_async_copy(vw.at[0], w.at[f, 1], own_sem.at[1])
    own_k.start()
    own_v.start()

    targets = (
        (o > 0, index(o - 1, i, core)),
        (o < outer - 1, index(o + 1, i, core)),
        (i > 0, index(o, i - 1, core)),
        (i < inner - 1, index(o, i + 1, core)),
        (None, index(o, i, 1 - core)),
    )

    barrier = pltpu.get_barrier_semaphore()
    for cond, target in targets:
        def greet(target=target):
            pl.semaphore_signal(barrier, inc=1, device_id={"fsdp": target}, device_id_type=MESH)
        if cond is None:
            greet()
        else:
            pl.when(cond)(greet)
    for step in range(1, sections):
        pl.semaphore_signal(
            barrier, inc=1, device_id={"section": lax.rem(s + step, sections)}, device_id_type=MESH
        )
    expected = (
        jnp.where(o > 0, 1, 0) + jnp.where(o < outer - 1, 1, 0)
        + jnp.where(i > 0, 1, 0) + jnp.where(i < inner - 1, 1, 0) + sections
    )
    pl.semaphore_wait(barrier, expected)

    def w_copy(way, origin):
        return pltpu.make_async_remote_copy(
            src_ref=w.at[origin], dst_ref=w.at[origin],
            send_sem=w_send.at[way, origin], recv_sem=w_recv.at[origin],
            device_id={"fsdp": targets[way][1]}, device_id_type=MESH,
        )

    def w_start(way, origin):
        cond = targets[way][0]
        if cond is None:
            w_copy(way, origin).start()
        else:
            pl.when(cond)(lambda: w_copy(way, origin).start())

    own_k.wait()
    own_v.wait()
    for way in range(5):
        w_start(way, f)

    mine = pl.ds(pl.multiple_of(s * part, part), part)

    def hid_copy(to):
        dst = xs if to == 0 else xin
        return pltpu.make_async_remote_copy(
            src_ref=hid.at[0], dst_ref=dst.at[mine], send_sem=hid_send.at[to],
            recv_sem=hid_recv.at[s], device_id={"section": to}, device_id_type=MESH,
        )

    def hid_local(to):
        dst = xs if to == 0 else xin
        return pltpu.make_async_copy(hid.at[0], dst.at[mine], hid_own)

    for to in range(min(2, sections)):
        pl.when(s != to)(lambda to=to: hid_copy(to).start())
        pl.when(s == to)(lambda to=to: hid_local(to).start())

    q_copy = pltpu.make_async_remote_copy(
        src_ref=q_in.at[0, 0], dst_ref=qp, send_sem=q_sem.at[0], recv_sem=q_sem.at[1],
        device_id={"section": jnp.minimum(s + 1, sections - 1)}, device_id_type=MESH,
    )
    kv_copy = pltpu.make_async_remote_copy(
        src_ref=kv, dst_ref=kvp, send_sem=kv_sem.at[0], recv_sem=kv_sem.at[1],
        device_id={"section": jnp.minimum(s + 1, sections - 1)}, device_id_type=MESH,
    )
    x_copy = pltpu.make_async_remote_copy(
        src_ref=xs, dst_ref=xin, send_sem=x_sem.at[0], recv_sem=x_sem.at[1],
        device_id={"section": jnp.minimum(s + 1, sections - 1)}, device_id_type=MESH,
    )
    last = s == sections - 1
    pl.when(jnp.logical_not(last))(lambda: q_copy.start())

    q_load = pltpu.make_async_copy(q_in.at[0, 0], qs, own_sem.at[0])
    q_load.start()
    q_load.wait()

    def rope_queries(ref):
        def one(h, _):
            cols = pl.ds(pl.multiple_of(h * HD, HD), HD)
            u = ref[:, cols].astype(jnp.float32)
            ref[:, cols] = rope(u, cos_ref[...], sin_ref[...]).astype(jnp.bfloat16)
            return 0
        lax.fori_loop(0, width // HD, one, 0)

    rope_queries(qs)

    def hid_arrive(to):
        hid_local(to).wait()
        dst = xs if to == 0 else xin
        for step in range(1, sections):
            j = lax.rem(to + step, sections)
            pltpu.make_async_remote_copy(
                src_ref=hid.at[0], dst_ref=dst.at[pl.ds(j * part, part)],
                send_sem=hid_send.at[to], recv_sem=hid_recv.at[j],
                device_id={"section": to}, device_id_type=MESH,
            ).wait_recv()

    block = 16

    def norm():
        def one(r, _):
            at = pl.ds(pl.multiple_of(r * block, block), block)
            x = xs[at, :].astype(jnp.float32)
            mean_square = jnp.mean(x * x, axis=-1, keepdims=True)
            y = (x * lax.rsqrt(mean_square + EPS) * gain[...]).astype(jnp.bfloat16)
            for pair in range(n // 2):
                normed[pair, at, :] = y[:, pair * 2 * depth:(pair + 1) * 2 * depth]
            return 0
        lax.fori_loop(0, rows // block, one, 0)

    def project(pair):
        a = normed[pair]
        for half in range(2):
            b = w[pl.ds(pair * 2, 2), half].reshape(2 * depth, kvw)
            acc[half] += jnp.dot(a, b, preferred_element_type=jnp.float32)

    acc[...] = jnp.zeros_like(acc)

    def arrive(origin, ways):
        w_copy(4, origin).wait_recv()
        for way in ways:
            w_start(way, origin)

    def spread(t, c, t_in, receive):
        for sign, way in ((-1, 1), (1, 0)):
            far = o - t if sign < 0 else o + t
            there = (far >= 0) if sign < 0 else (far < outer)
            pl.when(there)(lambda far=far, way=way: receive(index(far, i, c), (way, 2, 3, 4)))

    def spread_inner(t, c, receive):
        for sign in (-1, 1):
            far = o - t if sign < 0 else o + t
            there = (far >= 0) if sign < 0 else ((far < outer) & (t > 0))
            for d in range(1, inner):
                pl.when(there & (i - d >= 0))(
                    lambda far=far, d=d: receive(index(far, i - d, c), (3, 4)))
                pl.when(there & (i + d < inner))(
                    lambda far=far, d=d: receive(index(far, i + d, c), (2, 4)))

    def from_other(origin, ways):
        arrive(origin, ())

    def project_pair(origin, ways):
        project(origin // 2)

    def step(t, _):
        spread(t + 1, core, t, arrive)

        @pl.when((t == 0) & (s == 0))
        def _():
            hid_arrive(0)
            norm()

        @pl.when(t == 0)
        def _():
            from_other(index(o, i, 1 - core), ())

        spread_inner(t, core, arrive)
        spread(t + 1, 1 - core, t, from_other)
        spread_inner(t, 1 - core, from_other)

        @pl.when(s == 0)
        def _():
            pl.when(t == 0)(lambda: project(chip))
            spread(t + 1, core, t, project_pair)
            spread_inner(t, core, project_pair)

        return 0

    lax.fori_loop(0, outer, step, 0)

    row = lax.broadcasted_iota(jnp.int32, (rows, rows), 0)
    col = lax.broadcasted_iota(jnp.int32, (rows, rows), 1)
    scale = math.log2(math.e) / math.sqrt(HD)

    def attend(q_ref, kv_ref, x_ref, o_write):
        ones = jnp.ones((rows, HD), jnp.bfloat16)
        allowed = (col <= row)[None]

        def one(g, _):
            at = pl.ds(pl.multiple_of(g * HD, HD), HD)
            k = kv_ref[0, :, at]
            v = jnp.concatenate([kv_ref[1, :, at], ones], axis=1)
            base = g * group * HD
            cols = [pl.ds(pl.multiple_of(base + h * HD, HD), HD) for h in range(group)]
            q = jnp.concatenate([q_ref[:, c] for c in cols], axis=0)
            scores = lax.dot_general(q, k, (((1,), (1,)), ((), ())), preferred_element_type=jnp.float32)
            scores = jnp.where(allowed, scores.reshape(group, rows, rows), -1e30)
            top = jnp.max(scores, axis=-1, keepdims=True)
            p = jnp.exp2((scores - top) * scale).astype(jnp.bfloat16).reshape(group * rows, rows)
            mixed = jnp.dot(p, v, preferred_element_type=jnp.float32)
            mixed = mixed[:, :HD] / mixed[:, HD:]
            for h in range(group):
                o_write(cols[h], (
                    x_ref[:, cols[h]].astype(jnp.float32) + mixed[h * rows:(h + 1) * rows]
                ).astype(jnp.bfloat16))
            return 0

        lax.fori_loop(0, kv_heads, one, 0)

    def write_xs(c, value):
        xs[:, c] = value

    def write_out(c, value):
        out[0, 0, :, c] = value

    @pl.when(s > 0)
    def _():
        q_copy.wait_recv()
        rope_queries(qp)
        pl.when(s == 1)(lambda: hid_arrive(1))
        if sections > 2:
            pl.when(s > 1)(lambda: x_copy.wait_recv())
        kv_copy.wait_recv()
        attend(qp, kvp, xin, write_xs)
        if sections > 2:
            pl.when(jnp.logical_not(last))(lambda: x_copy.start())
        norm()
        def one(j, _):
            project(j)
            return 0
        lax.fori_loop(0, n // 2, one, 0)

    for h in range(kv_heads):
        at = slice(h * HD, (h + 1) * HD)
        kv[0, :, at] = rope(acc[0, :, at], cos_ref[...], sin_ref[...]).astype(jnp.bfloat16)
    kv[1] = acc[1].astype(jnp.bfloat16)
    pl.when(jnp.logical_not(last))(lambda: kv_copy.start())
    attend(qs, kv, xs, write_out)

    def drain(origin, ways):
        for way in ways:
            cond = targets[way][0]
            if cond is None:
                w_copy(way, origin).wait_send()
            else:
                pl.when(cond)(lambda way=way: w_copy(way, origin).wait_send())

    drain(f, range(5))

    def drain_step(t, _):
        spread(t + 1, core, t, drain)
        spread_inner(t, core, drain)
        return 0

    lax.fori_loop(0, outer, drain_step, 0)
    for to in range(min(2, sections)):
        pl.when(s != to)(lambda to=to: hid_copy(to).wait_send())

    @pl.when(jnp.logical_not(last))
    def _():
        q_copy.wait_send()
        kv_copy.wait_send()
        if sections > 2:
            pl.when(s > 0)(lambda: x_copy.wait_send())


def solution(mesh):
    sections, n = mesh.shape["section"], mesh.shape["fsdp"]
    chips = n // 2
    outer = 4 if chips % 4 == 0 else 1
    inner = chips // outer

    def body(hidden_in, queries, key_weight, value_weight, norm_gain):
        rows, width = queries.shape[2:]
        depth, kvw = key_weight.shape[1:]
        cosine, sine = rope_tables(rows)
        hbm = pl.BlockSpec(memory_space=pl.ANY)
        vmem = pl.BlockSpec(memory_space=pltpu.VMEM)
        dma = pltpu.SemaphoreType.DMA
        bf16, f32 = jnp.bfloat16, jnp.float32
        return pl.pallas_call(
            functools.partial(kernel, n, sections, outer, inner),
            out_shape=jax.ShapeDtypeStruct(queries.shape, bf16),
            in_specs=[hbm] * 4 + [vmem] * 3,
            out_specs=vmem,
            scratch_shapes=[
                pltpu.VMEM((n, 2, depth, kvw), bf16),
                pltpu.VMEM((rows, width), bf16),
                pltpu.VMEM((rows, width), bf16),
                pltpu.VMEM((rows, width), bf16),
                pltpu.VMEM((rows, width), bf16),
                pltpu.VMEM((n // 2, rows, 2 * depth), bf16),
                pltpu.VMEM((2, rows, kvw), f32),
                pltpu.VMEM((2, rows, kvw), bf16),
                pltpu.VMEM((2, rows, kvw), bf16),
                dma((n,)), dma((5, n)), dma((2,)), dma((sections,)), dma((2,)), dma,
                dma((2,)), dma((2,)), dma((2,)),
            ],
            compiler_params=pltpu.CompilerParams(
                collective_id=0, has_side_effects=True, vmem_limit_bytes=56 * 2**20
            ),
        )(hidden_in, queries, key_weight, value_weight, norm_gain, jnp.asarray(cosine), jnp.asarray(sine))

    placed = (
        P("fsdp", "section", None),
        P("section", "fsdp", None, None),
        P("section", "fsdp", None),
        P("section", "fsdp", None),
        P("section", None),
    )
    return jax.shard_map(
        body, mesh=mesh, in_specs=placed, out_specs=P("section", "fsdp", None, None), check_vma=False
    )
```

```python
import functools
import math

import jax
import jax.numpy as jnp
import numpy as np
from jax import lax
from jax.experimental import pallas as pl
from jax.experimental.pallas import tpu as pltpu
from jax.sharding import PartitionSpec as P

HD = 128
EPS = 1e-05
MESH = pl.DeviceIdType.MESH


def rope_tables(rows):
    half = HD // 2
    frequency = np.exp(np.arange(half, dtype=np.float32) * np.float32(-2.0 * math.log(10000.0) / HD))
    angles = np.arange(rows, dtype=np.float32)[:, None] * frequency[None, :].astype(np.float32)
    cosine, sine = np.cos(angles), np.sin(angles)
    return (
        np.concatenate([cosine, cosine], 1).astype(np.float32),
        np.concatenate([-sine, sine], 1).astype(np.float32),
    )


def rope(u, cosine, sine):
    return u * cosine + pltpu.roll(u, HD // 2, 1) * sine


def kernel(
    n, sections, outer, inner,
    hid, q_in, kw, vw, gain_in, cos_in, sin_in,
    out,
    w, xin, xs, qs, qp, normed, acc, kv, kvp, gain, cos_ref, sin_ref,
    w_recv, w_send, own_sem, hid_recv, hid_send, hid_own, q_sem, kv_sem, x_sem, load_sem,
):
    s = lax.axis_index("section")
    f = lax.axis_index("fsdp")
    core = lax.rem(f, 2)
    chip = f // 2
    i = lax.rem(chip, inner)
    o = chip // inner
    rows, width = xs.shape
    part = hid.shape[1]
    kvw = kw.shape[2]
    kv_heads = kvw // HD
    group = width // kvw
    depth = kw.shape[1]

    def index(oo, ii, cc):
        return (oo * inner + ii) * 2 + cc

    own_k = pltpu.make_async_copy(kw.at[0], w.at[f, 0], own_sem.at[0])
    own_v = pltpu.make_async_copy(vw.at[0], w.at[f, 1], own_sem.at[1])
    own_k.start()
    own_v.start()
    loads = [
        pltpu.make_async_copy(src, dst, load_sem.at[at])
        for at, (src, dst) in enumerate(
            ((q_in.at[0, 0], qs), (gain_in, gain), (cos_in, cos_ref), (sin_in, sin_ref)))
    ]
    for load in loads:
        load.start()

    targets = (
        (o > 0, index(o - 1, i, core)),
        (o < outer - 1, index(o + 1, i, core)),
        (i > 0, index(o, i - 1, core)),
        (i < inner - 1, index(o, i + 1, core)),
        (None, index(o, i, 1 - core)),
    )

    barrier = pltpu.get_barrier_semaphore()
    for cond, target in targets:
        def greet(target=target):
            pl.semaphore_signal(barrier, inc=1, device_id={"fsdp": target}, device_id_type=MESH)
        if cond is None:
            greet()
        else:
            pl.when(cond)(greet)
    for step in range(1, sections):
        pl.semaphore_signal(
            barrier, inc=1, device_id={"section": lax.rem(s + step, sections)}, device_id_type=MESH
        )
    expected = (
        jnp.where(o > 0, 1, 0) + jnp.where(o < outer - 1, 1, 0)
        + jnp.where(i > 0, 1, 0) + jnp.where(i < inner - 1, 1, 0) + sections
    )
    pl.semaphore_wait(barrier, expected)

    few = max(16, depth // 8)
    cuts = (pl.ds(0, depth - few), pl.ds(depth - few, few))

    def w_copy(which, way, origin):
        piece = w.at[origin, :, cuts[which]]
        return pltpu.make_async_remote_copy(
            src_ref=piece, dst_ref=piece,
            send_sem=w_send.at[which, way, origin], recv_sem=w_recv.at[which, origin],
            device_id={"fsdp": targets[way][1]}, device_id_type=MESH,
        )

    def w_start(which, way, origin):
        cond = targets[way][0]
        if cond is None:
            w_copy(which, way, origin).start()
        else:
            pl.when(cond)(lambda: w_copy(which, way, origin).start())

    own_k.wait()
    own_v.wait()
    for way in (2, 3):
        w_start(1, way, f)
    for way in range(5):
        w_start(0, way, f)
    for way in (0, 1, 4):
        w_start(1, way, f)

    mine = pl.ds(pl.multiple_of(s * part, part), part)

    def hid_copy(to):
        dst = xs if to == 0 else xin
        return pltpu.make_async_remote_copy(
            src_ref=hid.at[0], dst_ref=dst.at[mine], send_sem=hid_send.at[to],
            recv_sem=hid_recv.at[s], device_id={"section": to}, device_id_type=MESH,
        )

    def hid_local(to):
        dst = xs if to == 0 else xin
        return pltpu.make_async_copy(hid.at[0], dst.at[mine], hid_own)

    for to in range(min(2, sections)):
        pl.when(s != to)(lambda to=to: hid_copy(to).start())
        pl.when(s == to)(lambda to=to: hid_local(to).start())

    q_copy = pltpu.make_async_remote_copy(
        src_ref=q_in.at[0, 0], dst_ref=qp, send_sem=q_sem.at[0], recv_sem=q_sem.at[1],
        device_id={"section": jnp.minimum(s + 1, sections - 1)}, device_id_type=MESH,
    )
    def kv_copy(g):
        return pltpu.make_async_remote_copy(
            src_ref=kv.at[g], dst_ref=kvp.at[g], send_sem=kv_sem.at[0, g], recv_sem=kv_sem.at[1, g],
            device_id={"section": jnp.minimum(s + 1, sections - 1)}, device_id_type=MESH,
        )

    x_copy = pltpu.make_async_remote_copy(
        src_ref=xs, dst_ref=xin, send_sem=x_sem.at[0], recv_sem=x_sem.at[1],
        device_id={"section": jnp.minimum(s + 1, sections - 1)}, device_id_type=MESH,
    )
    last = s == sections - 1
    pl.when(jnp.logical_not(last))(lambda: q_copy.start())

    for load in loads:
        load.wait()

    def rope_queries(ref):
        def one(h, _):
            cols = pl.ds(pl.multiple_of(h * HD, HD), HD)
            u = ref[:, cols].astype(jnp.float32)
            ref[:, cols] = rope(u, cos_ref[...], sin_ref[...]).astype(jnp.bfloat16)
            return 0
        lax.fori_loop(0, width // HD, one, 0)

    rope_queries(qs)

    def hid_arrive(to):
        hid_local(to).wait()
        dst = xs if to == 0 else xin
        for step in range(1, sections):
            j = lax.rem(to + step, sections)
            pltpu.make_async_remote_copy(
                src_ref=hid.at[0], dst_ref=dst.at[pl.ds(j * part, part)],
                send_sem=hid_send.at[to], recv_sem=hid_recv.at[j],
                device_id={"section": to}, device_id_type=MESH,
            ).wait_recv()

    block = 16

    def norm():
        def one(r, _):
            at = pl.ds(pl.multiple_of(r * block, block), block)
            x = xs[at, :].astype(jnp.float32)
            mean_square = jnp.mean(x * x, axis=-1, keepdims=True)
            y = (x * lax.rsqrt(mean_square + EPS) * gain[...]).astype(jnp.bfloat16)
            for pair in range(n // 2):
                normed[pair, at, :] = y[:, pair * 2 * depth:(pair + 1) * 2 * depth]
            return 0
        lax.fori_loop(0, rows // block, one, 0)

    def project(pair):
        a = normed[pair]
        for half in range(2):
            b = w[pl.ds(pair * 2, 2), half].reshape(2 * depth, kvw)
            acc[half] += jnp.dot(a, b, preferred_element_type=jnp.float32)

    acc[...] = jnp.zeros_like(acc)

    def arrive(which, origin, ways):
        w_copy(which, 4, origin).wait_recv()
        for way in ways:
            w_start(which, way, origin)

    def relay(which, origin, ways):
        arrive(which, origin, ways)

    def from_other(which, origin, ways):
        arrive(which, origin, ())

    def project_pair(which, origin, ways):
        if which == 0:
            project(origin // 2)

    def sides(t, act):
        for sign, way in ((-1, 1), (1, 0)):
            far = o - t if sign < 0 else o + t
            there = (far >= 0) if sign < 0 else ((far < outer) & (t > 0))
            act(far, there, way)

    def around(there, act):
        for d in range(1, inner):
            pl.when(there & (i - d >= 0))(lambda d=d: act(i - d, 3))
            pl.when(there & (i + d < inner))(lambda d=d: act(i + d, 2))

    def along_outer(t, c, receive):
        def act(far, there, way):
            pl.when(there)(lambda: receive(0, index(far, i, c), (way, 2, 3, 4)))
            pl.when(there)(lambda: receive(1, index(far, i, c), (way, 4)))
            around(there, lambda ii, _: receive(1, index(far, ii, c), (way, 4)))
        sides(t, act)

    def along_inner(t, c, receive):
        def act(far, there, _):
            around(there, lambda ii, way: receive(0, index(far, ii, c), (way, 4)))
        sides(t, act)

    def first_inner(c, receive):
        around(o >= 0, lambda ii, way: receive(1, index(o, ii, c), (way, 0, 1, 4)))

    first_inner(core, relay)

    def step(t, _):
        along_outer(t + 1, core, relay)

        @pl.when((t == 0) & (s == 0))
        def _():
            hid_arrive(0)
            norm()

        @pl.when(t == 0)
        def _():
            for which in range(2):
                arrive(which, index(o, i, 1 - core), ())
            first_inner(1 - core, from_other)

        along_inner(t, core, relay)
        along_outer(t + 1, 1 - core, from_other)
        along_inner(t, 1 - core, from_other)

        @pl.when(s == 0)
        def _():
            pl.when(t == 0)(lambda: project(chip))
            along_outer(t + 1, core, project_pair)
            along_inner(t, core, project_pair)

        return 0

    lax.fori_loop(0, outer, step, 0)

    row = lax.broadcasted_iota(jnp.int32, (rows, rows), 0)
    col = lax.broadcasted_iota(jnp.int32, (rows, rows), 1)
    scale = math.log2(math.e) / math.sqrt(HD)

    def attend(q_ref, kv_ref, x_ref, o_write, ready):
        ones = jnp.ones((rows, HD), jnp.bfloat16)
        allowed = (col <= row)[None]

        def one(g, _):
            ready(g)
            k = kv_ref[g, 0]
            v = jnp.concatenate([kv_ref[g, 1], ones], axis=1)
            base = g * group * HD
            cols = [pl.ds(pl.multiple_of(base + h * HD, HD), HD) for h in range(group)]
            q = jnp.concatenate([q_ref[:, c] for c in cols], axis=0)
            scores = lax.dot_general(q, k, (((1,), (1,)), ((), ())), preferred_element_type=jnp.float32)
            scores = jnp.where(allowed, scores.reshape(group, rows, rows), -1e30)
            top = jnp.max(scores, axis=-1, keepdims=True)
            p = jnp.exp2((scores - top) * scale).astype(jnp.bfloat16).reshape(group * rows, rows)
            mixed = jnp.dot(p, v, preferred_element_type=jnp.float32)
            mixed = mixed[:, :HD] / mixed[:, HD:]
            for h in range(group):
                o_write(cols[h], (
                    x_ref[:, cols[h]].astype(jnp.float32) + mixed[h * rows:(h + 1) * rows]
                ).astype(jnp.bfloat16))
            return 0

        lax.fori_loop(0, kv_heads, one, 0)

    def write_xs(c, value):
        xs[:, c] = value

    def write_out(c, value):
        out[0, 0, :, c] = value

    @pl.when(s > 0)
    def _():
        q_copy.wait_recv()
        rope_queries(qp)
        pl.when(s == 1)(lambda: hid_arrive(1))
        if sections > 2:
            pl.when(s > 1)(lambda: x_copy.wait_recv())
        attend(qp, kvp, xin, write_xs, lambda g: kv_copy(g).wait_recv())
        if sections > 2:
            pl.when(jnp.logical_not(last))(lambda: x_copy.start())
        norm()
        def one(j, _):
            project(j)
            return 0
        lax.fori_loop(0, n // 2, one, 0)

    for h in range(kv_heads):
        at = slice(h * HD, (h + 1) * HD)
        kv[h, 0] = rope(acc[0, :, at], cos_ref[...], sin_ref[...]).astype(jnp.bfloat16)
        kv[h, 1] = acc[1, :, at].astype(jnp.bfloat16)
        pl.when(jnp.logical_not(last))(lambda h=h: kv_copy(h).start())
    attend(qs, kv, xs, write_out, lambda g: None)

    def drain(which, origin, ways):
        for way in ways:
            cond = targets[way][0]
            if cond is None:
                w_copy(which, way, origin).wait_send()
            else:
                pl.when(cond)(lambda way=way: w_copy(which, way, origin).wait_send())

    for which in range(2):
        drain(which, f, range(5))
    first_inner(core, drain)

    def drain_step(t, _):
        along_outer(t + 1, core, drain)
        along_inner(t, core, drain)
        return 0

    lax.fori_loop(0, outer, drain_step, 0)
    for to in range(min(2, sections)):
        pl.when(s != to)(lambda to=to: hid_copy(to).wait_send())

    @pl.when(jnp.logical_not(last))
    def _():
        q_copy.wait_send()
        for h in range(kv_heads):
            kv_copy(h).wait_send()
        if sections > 2:
            pl.when(s > 0)(lambda: x_copy.wait_send())


def solution(mesh):
    sections, n = mesh.shape["section"], mesh.shape["fsdp"]
    chips = n // 2
    outer = 4 if chips % 4 == 0 else 1
    inner = chips // outer

    def body(hidden_in, queries, key_weight, value_weight, norm_gain):
        rows, width = queries.shape[2:]
        depth, kvw = key_weight.shape[1:]
        cosine, sine = rope_tables(rows)
        hbm = pl.BlockSpec(memory_space=pltpu.HBM)
        vmem = pl.BlockSpec(memory_space=pltpu.VMEM)
        dma = pltpu.SemaphoreType.DMA
        bf16, f32 = jnp.bfloat16, jnp.float32
        return pl.pallas_call(
            functools.partial(kernel, n, sections, outer, inner),
            out_shape=jax.ShapeDtypeStruct(queries.shape, bf16),
            in_specs=[hbm] * 7,
            out_specs=vmem,
            scratch_shapes=[
                pltpu.VMEM((n, 2, depth, kvw), bf16),
                pltpu.VMEM((rows, width), bf16),
                pltpu.VMEM((rows, width), bf16),
                pltpu.VMEM((rows, width), bf16),
                pltpu.VMEM((rows, width), bf16),
                pltpu.VMEM((n // 2, rows, 2 * depth), bf16),
                pltpu.VMEM((2, rows, kvw), f32),
                pltpu.VMEM((kvw // HD, 2, rows, HD), bf16),
                pltpu.VMEM((kvw // HD, 2, rows, HD), bf16),
                pltpu.VMEM((1, width), f32),
                pltpu.VMEM((rows, HD), f32),
                pltpu.VMEM((rows, HD), f32),
                dma((2, n)), dma((2, 5, n)), dma((2,)), dma((sections,)), dma((2,)), dma,
                dma((2,)), dma((2, kvw // HD)), dma((2,)), dma((4,)),
            ],
            compiler_params=pltpu.CompilerParams(
                collective_id=0, has_side_effects=True, vmem_limit_bytes=28 * 2**20
            ),
        )(hidden_in, queries, key_weight, value_weight, norm_gain, jnp.asarray(cosine), jnp.asarray(sine))

    placed = (
        P("fsdp", "section", None),
        P("section", "fsdp", None, None),
        P("section", "fsdp", None),
        P("section", "fsdp", None),
        P("section", None),
    )
    return jax.shard_map(
        body, mesh=mesh, in_specs=placed, out_specs=P("section", "fsdp", None, None), check_vma=False
    )
```

```python
import functools
import math

import jax
import jax.numpy as jnp
import numpy as np
from jax import lax
from jax.experimental import pallas as pl
from jax.experimental.pallas import tpu as pltpu
from jax.sharding import PartitionSpec as P

HD = 128
EPS = 1e-05
MESH = pl.DeviceIdType.MESH


def rope_tables(rows):
    half = HD // 2
    frequency = np.exp(np.arange(half, dtype=np.float32) * np.float32(-2.0 * math.log(10000.0) / HD))
    angles = np.arange(rows, dtype=np.float32)[:, None] * frequency[None, :].astype(np.float32)
    cosine, sine = np.cos(angles), np.sin(angles)
    return (
        np.concatenate([cosine, cosine], 1).astype(np.float32),
        np.concatenate([-sine, sine], 1).astype(np.float32),
    )


def rope(u, cosine, sine):
    return u * cosine + pltpu.roll(u, HD // 2, 1) * sine


def kernel(
    n, sections, outer, inner,
    hid, q_in, kw, vw, gain_in, cos_in, sin_in,
    out,
    w, xin, xs, qs, qp, normed, acc, kv, kvp, gain, cos_ref, sin_ref,
    w_recv, w_send, own_sem, hid_recv, hid_send, hid_own, q_sem, kv_sem, x_sem, load_sem,
):
    s = lax.axis_index("section")
    f = lax.axis_index("fsdp")
    core = lax.rem(f, 2)
    chip = f // 2
    i = lax.rem(chip, inner)
    o = chip // inner
    rows, width = xs.shape
    part = hid.shape[1]
    kvw = kw.shape[2]
    kv_heads = kvw // HD
    group = width // kvw
    depth = kw.shape[1]

    def index(oo, ii, cc):
        return (oo * inner + ii) * 2 + cc

    own_k = pltpu.make_async_copy(kw.at[0], w.at[f, 0], own_sem.at[0])
    own_v = pltpu.make_async_copy(vw.at[0], w.at[f, 1], own_sem.at[1])
    own_k.start()
    own_v.start()
    loads = [
        pltpu.make_async_copy(src, dst, load_sem.at[at])
        for at, (src, dst) in enumerate(
            ((q_in.at[0, 0], qs), (gain_in, gain), (cos_in, cos_ref), (sin_in, sin_ref)))
    ]
    for load in loads:
        load.start()

    targets = (
        (o > 0, index(o - 1, i, core)),
        (o < outer - 1, index(o + 1, i, core)),
        (i > 0, index(o, i - 1, core)),
        (i < inner - 1, index(o, i + 1, core)),
        (None, index(o, i, 1 - core)),
    )

    barrier = pltpu.get_barrier_semaphore()
    for cond, target in targets:
        def greet(target=target):
            pl.semaphore_signal(barrier, inc=1, device_id={"fsdp": target}, device_id_type=MESH)
        if cond is None:
            greet()
        else:
            pl.when(cond)(greet)
    for step in range(1, sections):
        pl.semaphore_signal(
            barrier, inc=1, device_id={"section": lax.rem(s + step, sections)}, device_id_type=MESH
        )
    expected = (
        jnp.where(o > 0, 1, 0) + jnp.where(o < outer - 1, 1, 0)
        + jnp.where(i > 0, 1, 0) + jnp.where(i < inner - 1, 1, 0) + sections
    )
    pl.semaphore_wait(barrier, expected)

    few = max(16, depth // 8)
    first = (depth - few + 16) // 32 * 16
    cuts = (pl.ds(0, first), pl.ds(first, depth - few - first), pl.ds(depth - few, few))
    mains, tail = (0, 1), 2

    def w_copy(which, way, origin):
        piece = w.at[origin, :, cuts[which]]
        return pltpu.make_async_remote_copy(
            src_ref=piece, dst_ref=piece,
            send_sem=w_send.at[which, way, origin], recv_sem=w_recv.at[which, origin],
            device_id={"fsdp": targets[way][1]}, device_id_type=MESH,
        )

    def w_start(which, way, origin):
        cond = targets[way][0]
        if cond is None:
            w_copy(which, way, origin).start()
        else:
            pl.when(cond)(lambda: w_copy(which, way, origin).start())

    own_k.wait()
    own_v.wait()
    for way in (2, 3):
        w_start(tail, way, f)
    for which in mains:
        for way in range(5):
            w_start(which, way, f)
    for way in (0, 1, 4):
        w_start(tail, way, f)

    mine = pl.ds(pl.multiple_of(s * part, part), part)

    def hid_copy(to):
        dst = xs if to == 0 else xin
        return pltpu.make_async_remote_copy(
            src_ref=hid.at[0], dst_ref=dst.at[mine], send_sem=hid_send.at[to],
            recv_sem=hid_recv.at[s], device_id={"section": to}, device_id_type=MESH,
        )

    def hid_local(to):
        dst = xs if to == 0 else xin
        return pltpu.make_async_copy(hid.at[0], dst.at[mine], hid_own)

    for to in range(min(2, sections)):
        pl.when(s != to)(lambda to=to: hid_copy(to).start())
        pl.when(s == to)(lambda to=to: hid_local(to).start())

    q_copy = pltpu.make_async_remote_copy(
        src_ref=q_in.at[0, 0], dst_ref=qp, send_sem=q_sem.at[0], recv_sem=q_sem.at[1],
        device_id={"section": jnp.minimum(s + 1, sections - 1)}, device_id_type=MESH,
    )
    def kv_copy(g):
        return pltpu.make_async_remote_copy(
            src_ref=kv.at[g], dst_ref=kvp.at[g], send_sem=kv_sem.at[0, g], recv_sem=kv_sem.at[1, g],
            device_id={"section": jnp.minimum(s + 1, sections - 1)}, device_id_type=MESH,
        )

    x_copy = pltpu.make_async_remote_copy(
        src_ref=xs, dst_ref=xin, send_sem=x_sem.at[0], recv_sem=x_sem.at[1],
        device_id={"section": jnp.minimum(s + 1, sections - 1)}, device_id_type=MESH,
    )
    last = s == sections - 1
    pl.when(jnp.logical_not(last))(lambda: q_copy.start())

    for load in loads:
        load.wait()

    def rope_queries(ref):
        def one(h, _):
            cols = pl.ds(pl.multiple_of(h * HD, HD), HD)
            u = ref[:, cols].astype(jnp.float32)
            ref[:, cols] = rope(u, cos_ref[...], sin_ref[...]).astype(jnp.bfloat16)
            return 0
        lax.fori_loop(0, width // HD, one, 0)

    rope_queries(qs)

    def hid_arrive(to):
        hid_local(to).wait()
        dst = xs if to == 0 else xin
        for step in range(1, sections):
            j = lax.rem(to + step, sections)
            pltpu.make_async_remote_copy(
                src_ref=hid.at[0], dst_ref=dst.at[pl.ds(j * part, part)],
                send_sem=hid_send.at[to], recv_sem=hid_recv.at[j],
                device_id={"section": to}, device_id_type=MESH,
            ).wait_recv()

    block = 16

    def norm():
        def one(r, _):
            at = pl.ds(pl.multiple_of(r * block, block), block)
            x = xs[at, :].astype(jnp.float32)
            mean_square = jnp.mean(x * x, axis=-1, keepdims=True)
            y = (x * lax.rsqrt(mean_square + EPS) * gain[...]).astype(jnp.bfloat16)
            for pair in range(n // 2):
                normed[pair, at, :] = y[:, pair * 2 * depth:(pair + 1) * 2 * depth]
            return 0
        lax.fori_loop(0, rows // block, one, 0)

    def project(pair):
        a = normed[pair]
        for half in range(2):
            b = w[pl.ds(pair * 2, 2), half].reshape(2 * depth, kvw)
            acc[half] += jnp.dot(a, b, preferred_element_type=jnp.float32)

    acc[...] = jnp.zeros_like(acc)

    def arrive(which, origin, ways):
        w_copy(which, 4, origin).wait_recv()
        for way in ways:
            w_start(which, way, origin)

    def relay(which, origin, ways):
        arrive(which, origin, ways)

    def from_other(which, origin, ways):
        arrive(which, origin, ())

    def project_pair(which, origin, ways):
        if which == tail - 1:
            project(origin // 2)

    def sides(t, act):
        for sign, way in ((-1, 1), (1, 0)):
            far = o - t if sign < 0 else o + t
            there = (far >= 0) if sign < 0 else ((far < outer) & (t > 0))
            act(far, there, way)

    def around(there, act):
        for d in range(1, inner):
            pl.when(there & (i - d >= 0))(lambda d=d: act(i - d, 3))
            pl.when(there & (i + d < inner))(lambda d=d: act(i + d, 2))

    def along_outer(t, c, receive):
        for which in mains:
            def act(far, there, way, which=which):
                pl.when(there)(lambda: receive(which, index(far, i, c), (way, 2, 3, 4)))
            sides(t, act)

        def act_tail(far, there, way):
            pl.when(there)(lambda: receive(tail, index(far, i, c), (way, 4)))
            around(there, lambda ii, _: receive(tail, index(far, ii, c), (way, 4)))
        sides(t, act_tail)

    def along_inner(t, c, receive):
        for which in mains:
            def act(far, there, _, which=which):
                around(there, lambda ii, way: receive(which, index(far, ii, c), (way, 4)))
            sides(t, act)

    def first_inner(c, receive):
        around(o >= 0, lambda ii, way: receive(tail, index(o, ii, c), (way, 0, 1, 4)))

    first_inner(core, relay)

    def step(t, _):
        along_outer(t + 1, core, relay)

        @pl.when((t == 0) & (s == 0))
        def _():
            hid_arrive(0)
            norm()

        @pl.when(t == 0)
        def _():
            for which in (*mains, tail):
                arrive(which, index(o, i, 1 - core), ())
            first_inner(1 - core, from_other)

        along_inner(t, core, relay)
        along_outer(t + 1, 1 - core, from_other)
        along_inner(t, 1 - core, from_other)

        @pl.when(s == 0)
        def _():
            pl.when(t == 0)(lambda: project(chip))
            along_outer(t + 1, core, project_pair)
            along_inner(t, core, project_pair)

        return 0

    lax.fori_loop(0, outer, step, 0)

    row = lax.broadcasted_iota(jnp.int32, (rows, rows), 0)
    col = lax.broadcasted_iota(jnp.int32, (rows, rows), 1)
    scale = math.log2(math.e) / math.sqrt(HD)

    def attend(q_ref, kv_ref, x_ref, o_write, ready):
        ones = jnp.ones((rows, HD), jnp.bfloat16)
        allowed = (col <= row)[None]

        def one(g, _):
            ready(g)
            k = kv_ref[g, 0]
            v = jnp.concatenate([kv_ref[g, 1], ones], axis=1)
            base = g * group * HD
            cols = [pl.ds(pl.multiple_of(base + h * HD, HD), HD) for h in range(group)]
            q = jnp.concatenate([q_ref[:, c] for c in cols], axis=0)
            scores = lax.dot_general(q, k, (((1,), (1,)), ((), ())), preferred_element_type=jnp.float32)
            scores = jnp.where(allowed, scores.reshape(group, rows, rows), -1e30)
            top = jnp.max(scores, axis=-1, keepdims=True)
            p = jnp.exp2((scores - top) * scale).astype(jnp.bfloat16).reshape(group * rows, rows)
            mixed = jnp.dot(p, v, preferred_element_type=jnp.float32)
            mixed = mixed[:, :HD] / mixed[:, HD:]
            for h in range(group):
                o_write(cols[h], (
                    x_ref[:, cols[h]].astype(jnp.float32) + mixed[h * rows:(h + 1) * rows]
                ).astype(jnp.bfloat16))
            return 0

        lax.fori_loop(0, kv_heads, one, 0)

    def write_xs(c, value):
        xs[:, c] = value

    def write_out(c, value):
        out[0, 0, :, c] = value

    @pl.when(s > 0)
    def _():
        q_copy.wait_recv()
        rope_queries(qp)
        pl.when(s == 1)(lambda: hid_arrive(1))
        if sections > 2:
            pl.when(s > 1)(lambda: x_copy.wait_recv())
        attend(qp, kvp, xin, write_xs, lambda g: kv_copy(g).wait_recv())
        if sections > 2:
            pl.when(jnp.logical_not(last))(lambda: x_copy.start())
        norm()
        def one(j, _):
            project(j)
            return 0
        lax.fori_loop(0, n // 2, one, 0)

    for h in range(kv_heads):
        at = slice(h * HD, (h + 1) * HD)
        kv[h, 0] = rope(acc[0, :, at], cos_ref[...], sin_ref[...]).astype(jnp.bfloat16)
        kv[h, 1] = acc[1, :, at].astype(jnp.bfloat16)
        pl.when(jnp.logical_not(last))(lambda h=h: kv_copy(h).start())
    attend(qs, kv, xs, write_out, lambda g: None)

    def drain(which, origin, ways):
        for way in ways:
            cond = targets[way][0]
            if cond is None:
                w_copy(which, way, origin).wait_send()
            else:
                pl.when(cond)(lambda way=way: w_copy(which, way, origin).wait_send())

    for which in (*mains, tail):
        drain(which, f, range(5))
    first_inner(core, drain)

    def drain_step(t, _):
        along_outer(t + 1, core, drain)
        along_inner(t, core, drain)
        return 0

    lax.fori_loop(0, outer, drain_step, 0)
    for to in range(min(2, sections)):
        pl.when(s != to)(lambda to=to: hid_copy(to).wait_send())

    @pl.when(jnp.logical_not(last))
    def _():
        q_copy.wait_send()
        for h in range(kv_heads):
            kv_copy(h).wait_send()
        if sections > 2:
            pl.when(s > 0)(lambda: x_copy.wait_send())


def solution(mesh):
    sections, n = mesh.shape["section"], mesh.shape["fsdp"]
    chips = n // 2
    outer = 4 if chips % 4 == 0 else 1
    inner = chips // outer

    def body(hidden_in, queries, key_weight, value_weight, norm_gain):
        rows, width = queries.shape[2:]
        depth, kvw = key_weight.shape[1:]
        cosine, sine = rope_tables(rows)
        hbm = pl.BlockSpec(memory_space=pltpu.HBM)
        vmem = pl.BlockSpec(memory_space=pltpu.VMEM)
        dma = pltpu.SemaphoreType.DMA
        bf16, f32 = jnp.bfloat16, jnp.float32
        return pl.pallas_call(
            functools.partial(kernel, n, sections, outer, inner),
            out_shape=jax.ShapeDtypeStruct(queries.shape, bf16),
            in_specs=[hbm] * 7,
            out_specs=vmem,
            scratch_shapes=[
                pltpu.VMEM((n, 2, depth, kvw), bf16),
                pltpu.VMEM((rows, width), bf16),
                pltpu.VMEM((rows, width), bf16),
                pltpu.VMEM((rows, width), bf16),
                pltpu.VMEM((rows, width), bf16),
                pltpu.VMEM((n // 2, rows, 2 * depth), bf16),
                pltpu.VMEM((2, rows, kvw), f32),
                pltpu.VMEM((kvw // HD, 2, rows, HD), bf16),
                pltpu.VMEM((kvw // HD, 2, rows, HD), bf16),
                pltpu.VMEM((1, width), f32),
                pltpu.VMEM((rows, HD), f32),
                pltpu.VMEM((rows, HD), f32),
                dma((3, n)), dma((3, 5, n)), dma((2,)), dma((sections,)), dma((2,)), dma,
                dma((2,)), dma((2, kvw // HD)), dma((2,)), dma((4,)),
            ],
            compiler_params=pltpu.CompilerParams(
                collective_id=0, has_side_effects=True, vmem_limit_bytes=28 * 2**20
            ),
        )(*(
            pltpu.with_memory_space_constraint(x, pltpu.HBM)
            for x in (hidden_in, queries, key_weight, value_weight, norm_gain, jnp.asarray(cosine), jnp.asarray(sine))
        ))

    placed = (
        P("fsdp", "section", None),
        P("section", "fsdp", None, None),
        P("section", "fsdp", None),
        P("section", "fsdp", None),
        P("section", None),
    )
    return jax.shard_map(
        body, mesh=mesh, in_specs=placed, out_specs=P("section", "fsdp", None, None), check_vma=False
    )
```

```python
import functools
import math

import jax
import jax.numpy as jnp
import numpy as np
from jax import lax
from jax.experimental import pallas as pl
from jax.experimental.pallas import tpu as pltpu
from jax.sharding import PartitionSpec as P

HD = 128
EPS = 1e-05
MESH = pl.DeviceIdType.MESH


def rope_tables(rows):
    half = HD // 2
    frequency = np.exp(np.arange(half, dtype=np.float32) * np.float32(-2.0 * math.log(10000.0) / HD))
    angles = np.arange(rows, dtype=np.float32)[:, None] * frequency[None, :].astype(np.float32)
    cosine, sine = np.cos(angles), np.sin(angles)
    return (
        np.concatenate([cosine, cosine], 1).astype(np.float32),
        np.concatenate([-sine, sine], 1).astype(np.float32),
    )


def rope(u, cosine, sine):
    return u * cosine + pltpu.roll(u, HD // 2, 1) * sine


def kernel(
    n, sections, outer, inner,
    hid, q_in, kw, vw, gain_in, cos_in, sin_in,
    out,
    w, xin, xs, qs, qp, normed, acc, kv, kvp, gain, cos_ref, sin_ref,
    w_recv, w_send, own_sem, hid_recv, hid_send, hid_own, q_sem, kv_sem, x_sem, load_sem,
):
    s = lax.axis_index("section")
    f = lax.axis_index("fsdp")
    core = lax.rem(f, 2)
    chip = f // 2
    i = lax.rem(chip, inner)
    o = chip // inner
    rows, width = xs.shape
    part = hid.shape[1]
    kvw = kw.shape[2]
    kv_heads = kvw // HD
    group = width // kvw
    depth = kw.shape[1]

    def index(oo, ii, cc):
        return (oo * inner + ii) * 2 + cc

    own_k = pltpu.make_async_copy(kw.at[0], w.at[f, 0], own_sem.at[0])
    own_v = pltpu.make_async_copy(vw.at[0], w.at[f, 1], own_sem.at[1])
    own_k.start()
    own_v.start()
    loads = [
        pltpu.make_async_copy(src, dst, load_sem.at[at])
        for at, (src, dst) in enumerate(
            ((q_in.at[0, 0], qs), (gain_in, gain), (cos_in, cos_ref), (sin_in, sin_ref)))
    ]
    for load in loads:
        load.start()

    targets = (
        (o > 0, index(o - 1, i, core)),
        (o < outer - 1, index(o + 1, i, core)),
        (i > 0, index(o, i - 1, core)),
        (i < inner - 1, index(o, i + 1, core)),
        (None, index(o, i, 1 - core)),
    )

    barrier = pltpu.get_barrier_semaphore()
    for cond, target in targets:
        def greet(target=target):
            pl.semaphore_signal(barrier, inc=1, device_id={"fsdp": target}, device_id_type=MESH)
        if cond is None:
            greet()
        else:
            pl.when(cond)(greet)
    for step in range(1, sections):
        pl.semaphore_signal(
            barrier, inc=1, device_id={"section": lax.rem(s + step, sections)}, device_id_type=MESH
        )
    expected = (
        jnp.where(o > 0, 1, 0) + jnp.where(o < outer - 1, 1, 0)
        + jnp.where(i > 0, 1, 0) + jnp.where(i < inner - 1, 1, 0) + sections
    )
    pl.semaphore_wait(barrier, expected)

    few = max(16, depth // 8)
    third = (depth - few + 32) // 48 * 16
    edges = (0, third, 2 * third, depth - few, depth)
    cuts = tuple(pl.ds(a, b - a) for a, b in zip(edges[:-1], edges[1:]))
    mains, tail = (0, 1, 2), 3

    def w_copy(which, way, origin):
        piece = w.at[origin, :, cuts[which]]
        return pltpu.make_async_remote_copy(
            src_ref=piece, dst_ref=piece,
            send_sem=w_send.at[which, way, origin], recv_sem=w_recv.at[which, origin],
            device_id={"fsdp": targets[way][1]}, device_id_type=MESH,
        )

    def w_start(which, way, origin):
        cond = targets[way][0]
        if cond is None:
            w_copy(which, way, origin).start()
        else:
            pl.when(cond)(lambda: w_copy(which, way, origin).start())

    own_k.wait()
    own_v.wait()
    for way in (2, 3):
        w_start(tail, way, f)
    for which in mains:
        for way in range(5):
            w_start(which, way, f)
    for way in (0, 1, 4):
        w_start(tail, way, f)

    mine = pl.ds(pl.multiple_of(s * part, part), part)

    def hid_copy(to):
        dst = xs if to == 0 else xin
        return pltpu.make_async_remote_copy(
            src_ref=hid.at[0], dst_ref=dst.at[mine], send_sem=hid_send.at[to],
            recv_sem=hid_recv.at[s], device_id={"section": to}, device_id_type=MESH,
        )

    def hid_local(to):
        dst = xs if to == 0 else xin
        return pltpu.make_async_copy(hid.at[0], dst.at[mine], hid_own)

    for to in range(min(2, sections)):
        pl.when(s != to)(lambda to=to: hid_copy(to).start())
        pl.when(s == to)(lambda to=to: hid_local(to).start())

    q_copy = pltpu.make_async_remote_copy(
        src_ref=q_in.at[0, 0], dst_ref=qp, send_sem=q_sem.at[0], recv_sem=q_sem.at[1],
        device_id={"section": jnp.minimum(s + 1, sections - 1)}, device_id_type=MESH,
    )
    def kv_copy(g):
        return pltpu.make_async_remote_copy(
            src_ref=kv.at[g], dst_ref=kvp.at[g], send_sem=kv_sem.at[0, g], recv_sem=kv_sem.at[1, g],
            device_id={"section": jnp.minimum(s + 1, sections - 1)}, device_id_type=MESH,
        )

    x_copy = pltpu.make_async_remote_copy(
        src_ref=xs, dst_ref=xin, send_sem=x_sem.at[0], recv_sem=x_sem.at[1],
        device_id={"section": jnp.minimum(s + 1, sections - 1)}, device_id_type=MESH,
    )
    last = s == sections - 1
    pl.when(jnp.logical_not(last))(lambda: q_copy.start())

    for load in loads:
        load.wait()

    def rope_queries(ref):
        def one(h, _):
            cols = pl.ds(pl.multiple_of(h * HD, HD), HD)
            u = ref[:, cols].astype(jnp.float32)
            ref[:, cols] = rope(u, cos_ref[...], sin_ref[...]).astype(jnp.bfloat16)
            return 0
        lax.fori_loop(0, width // HD, one, 0)

    rope_queries(qs)

    def hid_arrive(to):
        hid_local(to).wait()
        dst = xs if to == 0 else xin
        for step in range(1, sections):
            j = lax.rem(to + step, sections)
            pltpu.make_async_remote_copy(
                src_ref=hid.at[0], dst_ref=dst.at[pl.ds(j * part, part)],
                send_sem=hid_send.at[to], recv_sem=hid_recv.at[j],
                device_id={"section": to}, device_id_type=MESH,
            ).wait_recv()

    block = 16

    def norm():
        def one(r, _):
            at = pl.ds(pl.multiple_of(r * block, block), block)
            x = xs[at, :].astype(jnp.float32)
            mean_square = jnp.mean(x * x, axis=-1, keepdims=True)
            y = (x * lax.rsqrt(mean_square + EPS) * gain[...]).astype(jnp.bfloat16)
            for pair in range(n // 2):
                normed[pair, at, :] = y[:, pair * 2 * depth:(pair + 1) * 2 * depth]
            return 0
        lax.fori_loop(0, rows // block, one, 0)

    def project(pair):
        a = normed[pair]
        for half in range(2):
            b = w[pl.ds(pair * 2, 2), half].reshape(2 * depth, kvw)
            acc[half] += jnp.dot(a, b, preferred_element_type=jnp.float32)

    acc[...] = jnp.zeros_like(acc)

    def arrive(which, origin, ways):
        w_copy(which, 4, origin).wait_recv()
        for way in ways:
            w_start(which, way, origin)

    def relay(which, origin, ways):
        arrive(which, origin, ways)

    def from_other(which, origin, ways):
        arrive(which, origin, ())

    def project_pair(which, origin, ways):
        if which == tail - 1:
            project(origin // 2)

    def sides(t, act):
        for sign, way in ((-1, 1), (1, 0)):
            far = o - t if sign < 0 else o + t
            there = (far >= 0) if sign < 0 else ((far < outer) & (t > 0))
            act(far, there, way)

    def around(there, act):
        for d in range(1, inner):
            pl.when(there & (i - d >= 0))(lambda d=d: act(i - d, 3))
            pl.when(there & (i + d < inner))(lambda d=d: act(i + d, 2))

    def along_outer(t, c, receive):
        for which in mains:
            def act(far, there, way, which=which):
                pl.when(there)(lambda: receive(which, index(far, i, c), (way, 2, 3, 4)))
            sides(t, act)

        def act_tail(far, there, way):
            pl.when(there)(lambda: receive(tail, index(far, i, c), (way, 4)))
            around(there, lambda ii, _: receive(tail, index(far, ii, c), (way, 4)))
        sides(t, act_tail)

    def along_inner(t, c, receive):
        for which in mains:
            def act(far, there, _, which=which):
                around(there, lambda ii, way: receive(which, index(far, ii, c), (way, 4)))
            sides(t, act)

    def first_inner(c, receive):
        around(o >= 0, lambda ii, way: receive(tail, index(o, ii, c), (way, 0, 1, 4)))

    first_inner(core, relay)

    def step(t, _):
        along_outer(t + 1, core, relay)

        @pl.when((t == 0) & (s == 0))
        def _():
            hid_arrive(0)
            norm()

        @pl.when(t == 0)
        def _():
            for which in (*mains, tail):
                arrive(which, index(o, i, 1 - core), ())
            first_inner(1 - core, from_other)

        along_inner(t, core, relay)
        along_outer(t + 1, 1 - core, from_other)
        along_inner(t, 1 - core, from_other)

        @pl.when(s == 0)
        def _():
            pl.when(t == 0)(lambda: project(chip))
            along_outer(t + 1, core, project_pair)
            along_inner(t, core, project_pair)

        return 0

    lax.fori_loop(0, outer, step, 0)

    row = lax.broadcasted_iota(jnp.int32, (rows, rows), 0)
    col = lax.broadcasted_iota(jnp.int32, (rows, rows), 1)
    scale = math.log2(math.e) / math.sqrt(HD)

    def attend(q_ref, kv_ref, x_ref, o_write, ready):
        ones = jnp.ones((rows, HD), jnp.bfloat16)
        allowed = (col <= row)[None]

        def one(g, _):
            ready(g)
            k = kv_ref[g, 0]
            v = jnp.concatenate([kv_ref[g, 1], ones], axis=1)
            base = g * group * HD
            cols = [pl.ds(pl.multiple_of(base + h * HD, HD), HD) for h in range(group)]
            q = jnp.concatenate([q_ref[:, c] for c in cols], axis=0)
            scores = lax.dot_general(q, k, (((1,), (1,)), ((), ())), preferred_element_type=jnp.float32)
            scores = jnp.where(allowed, scores.reshape(group, rows, rows), -1e30)
            top = jnp.max(scores, axis=-1, keepdims=True)
            p = jnp.exp2((scores - top) * scale).astype(jnp.bfloat16).reshape(group * rows, rows)
            mixed = jnp.dot(p, v, preferred_element_type=jnp.float32)
            mixed = mixed[:, :HD] / mixed[:, HD:]
            for h in range(group):
                o_write(cols[h], (
                    x_ref[:, cols[h]].astype(jnp.float32) + mixed[h * rows:(h + 1) * rows]
                ).astype(jnp.bfloat16))
            return 0

        lax.fori_loop(0, kv_heads, one, 0)

    def write_xs(c, value):
        xs[:, c] = value

    def write_out(c, value):
        out[0, 0, :, c] = value

    @pl.when(s > 0)
    def _():
        q_copy.wait_recv()
        rope_queries(qp)
        pl.when(s == 1)(lambda: hid_arrive(1))
        if sections > 2:
            pl.when(s > 1)(lambda: x_copy.wait_recv())
        attend(qp, kvp, xin, write_xs, lambda g: kv_copy(g).wait_recv())
        if sections > 2:
            pl.when(jnp.logical_not(last))(lambda: x_copy.start())
        norm()
        def one(j, _):
            project(j)
            return 0
        lax.fori_loop(0, n // 2, one, 0)

    for h in range(kv_heads):
        at = slice(h * HD, (h + 1) * HD)
        kv[h, 0] = rope(acc[0, :, at], cos_ref[...], sin_ref[...]).astype(jnp.bfloat16)
        kv[h, 1] = acc[1, :, at].astype(jnp.bfloat16)
        pl.when(jnp.logical_not(last))(lambda h=h: kv_copy(h).start())
    attend(qs, kv, xs, write_out, lambda g: None)

    def drain(which, origin, ways):
        for way in ways:
            cond = targets[way][0]
            if cond is None:
                w_copy(which, way, origin).wait_send()
            else:
                pl.when(cond)(lambda way=way: w_copy(which, way, origin).wait_send())

    for which in (*mains, tail):
        drain(which, f, range(5))
    first_inner(core, drain)

    def drain_step(t, _):
        along_outer(t + 1, core, drain)
        along_inner(t, core, drain)
        return 0

    lax.fori_loop(0, outer, drain_step, 0)
    for to in range(min(2, sections)):
        pl.when(s != to)(lambda to=to: hid_copy(to).wait_send())

    @pl.when(jnp.logical_not(last))
    def _():
        q_copy.wait_send()
        for h in range(kv_heads):
            kv_copy(h).wait_send()
        if sections > 2:
            pl.when(s > 0)(lambda: x_copy.wait_send())


def solution(mesh):
    sections, n = mesh.shape["section"], mesh.shape["fsdp"]
    chips = n // 2
    outer = 4 if chips % 4 == 0 else 1
    inner = chips // outer

    def body(hidden_in, queries, key_weight, value_weight, norm_gain):
        rows, width = queries.shape[2:]
        depth, kvw = key_weight.shape[1:]
        cosine, sine = rope_tables(rows)
        hbm = pl.BlockSpec(memory_space=pltpu.HBM)
        vmem = pl.BlockSpec(memory_space=pltpu.VMEM)
        dma = pltpu.SemaphoreType.DMA
        bf16, f32 = jnp.bfloat16, jnp.float32
        return pl.pallas_call(
            functools.partial(kernel, n, sections, outer, inner),
            out_shape=jax.ShapeDtypeStruct(queries.shape, bf16),
            in_specs=[hbm] * 7,
            out_specs=vmem,
            scratch_shapes=[
                pltpu.VMEM((n, 2, depth, kvw), bf16),
                pltpu.VMEM((rows, width), bf16),
                pltpu.VMEM((rows, width), bf16),
                pltpu.VMEM((rows, width), bf16),
                pltpu.VMEM((rows, width), bf16),
                pltpu.VMEM((n // 2, rows, 2 * depth), bf16),
                pltpu.VMEM((2, rows, kvw), f32),
                pltpu.VMEM((kvw // HD, 2, rows, HD), bf16),
                pltpu.VMEM((kvw // HD, 2, rows, HD), bf16),
                pltpu.VMEM((1, width), f32),
                pltpu.VMEM((rows, HD), f32),
                pltpu.VMEM((rows, HD), f32),
                dma((4, n)), dma((4, 5, n)), dma((2,)), dma((sections,)), dma((2,)), dma,
                dma((2,)), dma((2, kvw // HD)), dma((2,)), dma((4,)),
            ],
            compiler_params=pltpu.CompilerParams(
                collective_id=0, has_side_effects=True, vmem_limit_bytes=28 * 2**20
            ),
        )(*(
            pltpu.with_memory_space_constraint(x, pltpu.HBM)
            for x in (hidden_in, queries, key_weight, value_weight, norm_gain, jnp.asarray(cosine), jnp.asarray(sine))
        ))

    placed = (
        P("fsdp", "section", None),
        P("section", "fsdp", None, None),
        P("section", "fsdp", None),
        P("section", "fsdp", None),
        P("section", None),
    )
    return jax.shard_map(
        body, mesh=mesh, in_specs=placed, out_specs=P("section", "fsdp", None, None), check_vma=False
    )
```
